32 devices in a mesh: subj: 4 (over y, x), depth: 8 (over z, core).
Axes of the slice: x: 2, y: 2, z: 4, core: 2. Of those that a mesh axis runs over, the one named last changes fastest.
Arguments:
- images: float32 [4, 40, 128, 128], P('subj', 'depth'), may hold values from -6 to 6
- velocity: float32 [3, 4, 40, 128, 128], P(None, 'subj', 'depth'), may hold values from -3 to 3
- ref_index: int32 [4], replicated, may hold values from 0 to 3
- ref_weights: int32 [4, 4], P('subj'), may hold values from 0 to 16
Outputs:
- velocity_out: float32 [3, 4, 40, 128, 128], P(None, 'subj', 'depth')
The draws below stay inside these ranges and needn't reach their ends.
Inputs may be any that keep to these rules, and one draw needn't show every extreme that they name: `ref_index`: subject indices of the references; they may repeat. `ref_weights`: numerators over 16.
All inputs are finite; a program needn't handle non-finite values.
Results may differ from the reference program's by a relative error of at most 0.0003.
Values sent between devices are 32-bit elements; how exact they have to be, the bound alone decides.
No kernel may reach another device: no remote copies, remote signals or barrier semaphores. Data moves between devices by JAX's collectives and lax.ppermute only.
A program may use at most 64 MiB of HBM per device.

```python
import math
import jax
import jax.numpy as jnp
from jax import lax

X = 128
Y = 128
NREF = 4
WIN = 9
RG = 3
WDEN = 16
SUBJECTS = 4
Z = 40


def set_ends(entries, key, smallest, top_value):
    spot = [jax.random.randint(jax.random.fold_in(key, axis), (), 0, length) for axis, length in enumerate(entries.shape)]
    longest = entries.shape.index(max(entries.shape))
    beside = spot[:longest] + [(spot[longest] + 1) % entries.shape[longest]] + spot[longest + 1:]
    return entries.at[tuple(spot)].set(smallest).at[tuple(beside)].set(top_value)


def shard_levels(key, dims, cuts, low, largest):
    def one(axis_at, parts):
        draws = jax.random.uniform(jax.random.fold_in(jax.random.fold_in(key, 6), axis_at), (parts,), jnp.float32, low / len(cuts), largest / len(cuts))
        return jnp.repeat(jnp.exp(draws), dims[axis_at] // parts).reshape((-1,) + (1,) * (len(dims) - axis_at - 1))

    level = one(*cuts[0])
    for cut in cuts[1:]:
        level = level * one(*cut)
    return level


def gaussian(key, dims, spread, limit, shards=(), kind=jnp.bfloat16):
    values = jax.random.normal(key, dims, jnp.float32) * spread
    if len(shards) > 0:
        values = shard_levels(key, dims, shards, -0.22, 0.18) * values
    return jnp.clip(values, min=-limit, max=limit).astype(kind)


def setup_inputs(seed: int = 0) -> dict:
    keys = jax.random.split(jax.random.key(seed), 5)
    return {
        "images": gaussian(keys[0], (SUBJECTS, Z, X, Y), 1.0, 6.0, ((0, 4), (1, 8)), jnp.float32),
        "velocity": gaussian(keys[1], (3, SUBJECTS, Z, X, Y), 0.3, 3.0, ((1, 4), (2, 8)), jnp.float32),
        "ref_index": set_ends(jax.random.randint(keys[2], (NREF,), 0, SUBJECTS), jax.random.fold_in(keys[2], 1), 0, SUBJECTS - 1).astype(jnp.int32),
        "ref_weights": set_ends(jax.random.randint(keys[3], (SUBJECTS, NREF), 0, WDEN + 1), jax.random.fold_in(keys[3], 1), 0, WDEN).astype(jnp.int32),
    }


def gauss_taps():
    raw = [math.exp(-0.5 * offset * offset) for offset in range(-RG, RG + 1)]
    total = sum(raw)
    return [value / total for value in raw]


def window_sum(field, axis, taps):
    radius = len(taps) // 2
    widths = [(0, 0), (0, 0), (0, 0)]
    widths[axis] = (radius, radius)
    padded = jnp.pad(field, widths)
    length = field.shape[axis]
    total = taps[0] * lax.slice_in_dim(padded, 0, length, axis=axis)
    for offset in range(1, len(taps)):
        total = total + taps[offset] * lax.slice_in_dim(padded, offset, offset + length, axis=axis)
    return total


def filtered(field, taps):
    for axis in range(3):
        field = window_sum(field, axis, taps)
    return field


def boxed(field):
    return filtered(field, [1.0] * WIN) / float(WIN ** 3)


def central(field, axis):
    widths = [(0, 0), (0, 0), (0, 0)]
    widths[axis] = (1, 1)
    padded = jnp.pad(field, widths)
    length = field.shape[axis]
    upper = lax.slice_in_dim(padded, 2, length + 2, axis=axis)
    lower = lax.slice_in_dim(padded, 0, length, axis=axis)
    return (upper - lower) * 0.5


def reference(images, velocity, ref_index, ref_weights):
    taps = gauss_taps()

    def one_subject(inputs):
        moving, weights_row = inputs
        mean_i = boxed(moving)
        var_i = boxed(moving * moving) - mean_i * mean_i + 1e-5
        coeffs = jnp.zeros_like(moving)
        for refnum in range(NREF):
            fixed_img = images[ref_index[refnum]]
            mean_j = boxed(fixed_img)
            var_j = boxed(fixed_img * fixed_img) - mean_j * mean_j + 1e-5
            covariance = boxed(moving * fixed_img) - mean_i * mean_j
            term = 2.0 * covariance / (var_i * var_j) * ((fixed_img - mean_j) - covariance / var_i * (moving - mean_i))
            coeffs = coeffs + weights_row[refnum].astype(jnp.float32) / float(WDEN) * term
        return jnp.stack([filtered(coeffs * central(moving, axis), taps) for axis in range(3)])

    update = lax.map(one_subject, (images, ref_weights))
    return velocity + 40.0 * jnp.transpose(update, (1, 0, 2, 3, 4))
```

```python
import functools
import math

import jax
import jax.numpy as jnp
from jax import lax
from jax.experimental import pallas as pl
from jax.experimental.pallas import tpu as pltpu
from jax.sharding import PartitionSpec as P

WIN = 9
RAD = WIN // 2
RG = 3
WDEN = 16
STRIP = 16
PAD = 8


def gauss_taps():
    raw = [math.exp(-0.5 * offset * offset) for offset in range(-RG, RG + 1)]
    total = sum(raw)
    return [value / total for value in raw]


def band(size, taps, dtype):
    radius = len(taps) // 2
    rows = lax.broadcasted_iota(jnp.int32, (size, size), 0)
    cols = lax.broadcasted_iota(jnp.int32, (size, size), 1)
    gap = rows - cols
    matrix = jnp.zeros((size, size), jnp.float32)
    for offset, tap in enumerate(taps):
        matrix = jnp.where(gap == offset - radius, tap, matrix)
    return matrix.astype(dtype) if dtype is not None else matrix


def split3(value):
    hi = value.astype(jnp.bfloat16)
    rest = value - hi.astype(jnp.float32)
    mid = rest.astype(jnp.bfloat16)
    lo = (rest - mid.astype(jnp.float32)).astype(jnp.bfloat16)
    return hi, mid, lo


def depth_planes(refs, low_core, rows, reach):
    core, near, far = refs
    depth = core.shape[0]
    start = near.shape[0] - reach
    planes = [
        jnp.where(low_core, far[start + i, rows, :], near[start + i, rows, :])
        for i in range(reach)
    ]
    planes += [core[p, rows, :] for p in range(depth)]
    planes += [
        jnp.where(low_core, near[i, rows, :], far[i, rows, :]) for i in range(reach)
    ]
    return planes


def window_sums(planes, depth):
    reach = (len(planes) - depth) // 2
    if depth > 2 * reach + 1:
        return [sum(planes[p + 1 : p + 2 * reach + 1], planes[p]) for p in range(depth)]
    first, last = depth - 1, 2 * reach
    common = planes[first]
    for p in range(first + 1, last + 1):
        common = common + planes[p]
    left = [None] * depth
    run = None
    for p in range(first - 1, -1, -1):
        run = planes[p] if run is None else run + planes[p]
        left[p] = run
    right = [None] * depth
    run = None
    for p in range(last + 1, last + depth):
        run = planes[p] if run is None else run + planes[p]
        right[p - last] = run
    sums = []
    for p in range(depth):
        total = common
        if left[p] is not None:
            total = total + left[p]
        if right[p] is not None:
            total = total + right[p]
        sums.append(total)
    return sums


def clear_pads(sums_ref, width):
    count, _, lanes = sums_ref.shape
    zeros = jnp.zeros((count, PAD, lanes), jnp.float32)
    sums_ref[:, 0:PAD, :] = zeros
    sums_ref[:, PAD + width : 2 * PAD + width, :] = zeros


def box_strip(sums_ref, count, start, matrix):
    parts = []
    for f in range(count):
        total = sums_ref[f, pl.ds(start + PAD - RAD, STRIP), :]
        for k in range(1, WIN):
            total = total + sums_ref[f, pl.ds(start + PAD - RAD + k, STRIP), :]
        parts.append(total)
    stacked = jnp.concatenate(parts, axis=0)
    wide = jnp.concatenate(split3(stacked), axis=1)
    out = jnp.dot(wide, matrix, preferred_element_type=jnp.float32)
    out = out * (1.0 / float(WIN**3))
    return [out[f * STRIP : (f + 1) * STRIP, :] for f in range(count)]


def weight_of(index_ref, weights_ref, subject):
    total = jnp.int32(0)
    for r in range(index_ref.shape[0]):
        total = total + jnp.where(index_ref[r] == subject, weights_ref[0, r], 0)
    return total.astype(jnp.float32) / float(WDEN)


def box_matrix(size):
    one = band(size, [1.0] * WIN, jnp.bfloat16)
    return jnp.concatenate([one, one, one], axis=0)


def own_kernel(pick, core, near, far, *rest):
    index_ref, weights_ref, window_ref, mean_ref, inv_ref, acc_ref, grads_ref, sums_ref, wide_ref = rest
    depth, width, lanes = core.shape
    reach = depth + 2 * RG
    low_core = lax.axis_index("depth") % 2 == 0
    clear_pads(sums_ref, width)
    clear_pads(wide_ref, width)

    def gather(i, carry):
        start = pl.multiple_of(i * STRIP, STRIP)
        rows = pl.ds(start, STRIP)
        planes = depth_planes((core, near, far), low_core, rows, RAD)
        for p, value in enumerate(planes):
            window_ref[p, rows, :] = value
            wide_ref[p, pl.ds(start + PAD, STRIP), :] = value
        for f, field in enumerate((planes, [v * v for v in planes])):
            for p, total in enumerate(window_sums(field, depth)):
                sums_ref[f * depth + p, pl.ds(start + PAD, STRIP), :] = total
        return carry

    lax.fori_loop(0, width // STRIP, gather, 0)
    matrix = box_matrix(lanes)
    weight = jnp.float32(0.0)
    if pick is not None:
        weight = weight_of(index_ref, weights_ref, lax.axis_index("subj"))
    column = lax.broadcasted_iota(jnp.int32, (STRIP, lanes), 1)

    def finish(i, carry):
        start = pl.multiple_of(i * STRIP, STRIP)
        rows = pl.ds(start, STRIP)
        boxes = box_strip(sums_ref, 2 * depth, start, matrix)
        for p in range(depth):
            mean = boxes[p]
            cov = boxes[depth + p] - mean * mean
            inv = 1.0 / (cov + 1e-05)
            gap = core[p, rows, :] - mean
            ratio = cov * inv
            mean_ref[p, rows, :] = mean
            inv_ref[p, rows, :] = inv
            acc_ref[p, rows, :] = (weight * 2.0) * (ratio * inv) * (gap - ratio * gap)
        for p in range(reach):
            q = p + RAD - RG
            here = wide_ref[q, pl.ds(start + PAD, STRIP), :]
            above = wide_ref[q, pl.ds(start + PAD + 1, STRIP), :]
            below = wide_ref[q, pl.ds(start + PAD - 1, STRIP), :]
            front = wide_ref[q + 1, pl.ds(start + PAD, STRIP), :]
            back = wide_ref[q - 1, pl.ds(start + PAD, STRIP), :]
            right = jnp.where(column == lanes - 1, 0.0, pltpu.roll(here, lanes - 1, 1))
            left = jnp.where(column == 0, 0.0, pltpu.roll(here, 1, 1))
            grads_ref[p, rows, :] = (front - back) * 0.5
            grads_ref[reach + p, rows, :] = (above - below) * 0.5
            grads_ref[2 * reach + p, rows, :] = (right - left) * 0.5
        return carry

    lax.fori_loop(0, width // STRIP, finish, 0)


def pair_kernel(pick, last, jcore, jnear, jfar, window, mean_ref, inv_ref, acc_ref, index_ref, weights_ref, *rest):
    outs, sums_ref = rest[:-1], rest[-1]
    depth, width, lanes = jcore.shape
    low_core = lax.axis_index("depth") % 2 == 0
    if pick[0] == "xor":
        weight = weight_of(index_ref, weights_ref, lax.axis_index("subj") ^ pick[1])
    else:
        weight = weights_ref[0, pick[1]].astype(jnp.float32) / float(WDEN)
    clear_pads(sums_ref, width)

    def gather(i, carry):
        start = pl.multiple_of(i * STRIP, STRIP)
        rows = pl.ds(start, STRIP)
        mine = [window[p, rows, :] for p in range(depth + 2 * RAD)]
        planes = depth_planes((jcore, jnear, jfar), low_core, rows, RAD)
        fields = (planes, [v * v for v in planes], [a * b for a, b in zip(mine, planes)])
        for f, field in enumerate(fields):
            for p, total in enumerate(window_sums(field, depth)):
                sums_ref[f * depth + p, pl.ds(start + PAD, STRIP), :] = total
        return carry

    lax.fori_loop(0, width // STRIP, gather, 0)
    matrix = box_matrix(lanes)

    def finish(i, carry):
        start = pl.multiple_of(i * STRIP, STRIP)
        rows = pl.ds(start, STRIP)
        boxes = box_strip(sums_ref, 3 * depth, start, matrix)
        results = []
        for p in range(depth):
            mean_j = boxes[p]
            var_j = boxes[depth + p] - mean_j * mean_j + 1e-05
            mean_i = mean_ref[p, rows, :]
            inv_i = inv_ref[p, rows, :]
            cov = boxes[2 * depth + p] - mean_i * mean_j
            ratio = cov * inv_i
            gap = jcore[p, rows, :] - mean_j - ratio * (window[p + RAD, rows, :] - mean_i)
            term = (weight * 2.0) * ratio / var_j * gap
            results.append(acc_ref[p, rows, :] + term)
        for p in range(depth):
            outs[0][p, rows, :] = results[p]
        if last:
            for i in range(RG):
                low, high = results[i], results[depth - RG + i]
                outs[1][i, rows, :] = jnp.where(low_core, high, low)
                outs[2][i, rows, :] = jnp.where(low_core, low, high)
        return carry

    lax.fori_loop(0, width // STRIP, finish, 0)


def final_kernel(coeff, cnear, cfar, grads, velocity, out, force_ref, vel_ref, res_ref, in_sem, out_sem):
    depth, width, lanes = coeff.shape
    reach = depth + 2 * RG
    comps = 3
    load = pltpu.make_async_copy(velocity, vel_ref, in_sem)
    load.start()
    low_core = lax.axis_index("depth") % 2 == 0
    taps = gauss_taps()
    clear_pads(force_ref, width)

    def gather(i, carry):
        start = pl.multiple_of(i * STRIP, STRIP)
        rows = pl.ds(start, STRIP)
        weights = depth_planes((coeff, cnear, cfar), low_core, rows, RG)
        for f in range(comps):
            planes = [weights[p] * grads[f * reach + p, rows, :] for p in range(reach)]
            for p in range(depth):
                total = taps[RG] * planes[p + RG]
                for k in range(RG):
                    total = total + taps[k] * (planes[p + k] + planes[p + 2 * RG - k])
                force_ref[f * depth + p, pl.ds(start + PAD, STRIP), :] = total
        return carry

    lax.fori_loop(0, width // STRIP, gather, 0)
    full = band(lanes, taps, None)
    hi = full.astype(jnp.bfloat16)
    lo = (full - hi.astype(jnp.float32)).astype(jnp.bfloat16)
    matrix = jnp.concatenate([hi, hi, lo], axis=0)
    load.wait()

    def store(start, i):
        rows = pl.ds(start, STRIP)
        return pltpu.make_async_copy(res_ref.at[:, :, rows, :], out.at[:, 0, :, rows, :], out_sem.at[i])

    def finish(i, carry):
        start = pl.multiple_of(i * STRIP, STRIP)
        rows = pl.ds(start, STRIP)
        parts = []
        for f in range(comps * depth):
            rowed = [force_ref[f, pl.ds(start + PAD - RG + k, STRIP), :] for k in range(2 * RG + 1)]
            total = taps[RG] * rowed[RG]
            for k in range(RG):
                total = total + taps[k] * (rowed[k] + rowed[2 * RG - k])
            parts.append(total)
        stacked = jnp.concatenate(parts, axis=0)
        high = stacked.astype(jnp.bfloat16)
        low = (stacked - high.astype(jnp.float32)).astype(jnp.bfloat16)
        wide = jnp.concatenate([high, low, high], axis=1)
        smooth = jnp.dot(wide, matrix, preferred_element_type=jnp.float32)
        for f in range(comps):
            for p in range(depth):
                n = f * depth + p
                value = smooth[n * STRIP : (n + 1) * STRIP, :]
                res_ref[f, p, rows, :] = vel_ref[f, 0, p, rows, :] + 40.0 * value
        store(start, i).start()
        return carry

    lax.fori_loop(0, width // STRIP, finish, 0)
    for i in range(width // STRIP):
        store(i * STRIP, i).wait()


def f32(*shape):
    return jax.ShapeDtypeStruct(shape, jnp.float32)


def call(kernel, name, outs, scratch, n_vmem, n_smem, args, flops):
    whole = pl.BlockSpec(memory_space=pltpu.VMEM)
    small = pl.BlockSpec(memory_space=pltpu.SMEM)
    moved = sum(math.prod(a.shape) for a in args) + sum(math.prod(o.shape) for o in outs)
    return pl.pallas_call(
        kernel,
        name=name,
        out_shape=outs,
        in_specs=[whole] * n_vmem + [small] * n_smem,
        out_specs=[whole] * len(outs),
        scratch_shapes=scratch,
        cost_estimate=pl.CostEstimate(flops=flops, bytes_accessed=4 * moved, transcendentals=0),
    )(*args)


def on_device(images, velocity, ref_index, ref_weights):
    subjects = lax.axis_size("subj")
    stack = lax.axis_size("depth")
    own = images[0]
    depth, width, lanes = own.shape
    mate = [(i, i ^ 1) for i in range(stack)]
    hop = [(i, i + 2) for i in range(0, stack - 2, 2)] + [(i, i - 2) for i in range(3, stack, 2)]
    facing = [(i, i + 1) for i in range(1, stack - 1, 2)]
    facing = facing + [(j, i) for i, j in facing]

    def halos(slab):
        near = lax.ppermute(slab, "depth", mate)
        return near, lax.ppermute(near, "depth", hop)

    slabs = []
    if subjects <= ref_index.shape[0]:
        for k in range(1, subjects):
            swap = [(i, i ^ k) for i in range(subjects)]
            slabs.append((lax.ppermute(own, "subj", swap), ("xor", k)))
        self_pick = ("xor", 0)
    else:
        everyone = lax.all_gather(images, "subj", axis=0, tiled=True)
        for r in range(ref_index.shape[0]):
            slabs.append((everyone[ref_index[r]], ("ref", r)))
        self_pick = None

    near, far = halos(own)
    reach = depth + 2 * RG
    tall = width + 2 * PAD
    window, mean, inv, acc, grads = call(
        functools.partial(own_kernel, self_pick),
        "own",
        [f32(depth + 2 * RAD, width, lanes)] + [f32(depth, width, lanes)] * 3 + [f32(3 * reach, width, lanes)],
        [pltpu.VMEM((2 * depth, tall, lanes), jnp.float32), pltpu.VMEM((depth + 2 * RAD, tall, lanes), jnp.float32)],
        3,
        2,
        (own, near, far, ref_index, ref_weights),
        20_000_000,
    )
    for n, (slab, pick) in enumerate(slabs):
        last = n == len(slabs) - 1
        jnear, jfar = halos(slab)
        outs = [f32(depth, width, lanes)] + ([f32(RG, width, lanes)] * 2 if last else [])
        results = call(
            functools.partial(pair_kernel, pick, last),
            "pair",
            outs,
            [pltpu.VMEM((3 * depth, tall, lanes), jnp.float32)],
            7,
            2,
            (slab, jnear, jfar, window, mean, inv, acc, ref_index, ref_weights),
            20_000_000,
        )
        acc = results[0]
    cnear = lax.ppermute(results[1], "depth", mate)
    cfar = lax.ppermute(results[2], "depth", facing)
    whole = pl.BlockSpec(memory_space=pltpu.VMEM)
    away = pl.BlockSpec(memory_space=pl.ANY)
    return pl.pallas_call(
        final_kernel,
        name="smooth",
        out_shape=f32(3, 1, depth, width, lanes),
        in_specs=[whole] * 4 + [away],
        out_specs=away,
        scratch_shapes=[
            pltpu.VMEM((3 * depth, tall, lanes), jnp.float32),
            pltpu.VMEM((3, 1, depth, width, lanes), jnp.float32),
            pltpu.VMEM((3, depth, width, lanes), jnp.float32),
            pltpu.SemaphoreType.DMA,
            pltpu.SemaphoreType.DMA((width // STRIP,)),
        ],
        cost_estimate=pl.CostEstimate(flops=20_000_000, bytes_accessed=6_000_000, transcendentals=0),
    )(acc, cnear, cfar, grads, velocity)


def solution(mesh):
    placed = (
        P("subj", "depth", None, None),
        P(None, "subj", "depth", None, None),
        P(),
        P("subj", None),
    )
    return jax.shard_map(
        on_device,
        mesh=mesh,
        in_specs=placed,
        out_specs=P(None, "subj", "depth", None, None),
        check_vma=False,
    )
```
